32 devices in a mesh: lon: 8 (over z, x), lat: 4 (over y, core).
Axes of the slice: x: 2, y: 2, z: 4, core: 2. Of those that a mesh axis runs over, the one named last changes fastest.
Arguments:
- courant: float32 [4, 2, 137, 32, 512], P(None, None, None, 'lon', 'lat'), may hold values from -0.45 to 0.45
- slot_column_cells: int32 [4, 32, 32, 4], P(None, ('lon', 'lat')), may hold values from 0 to 511
- column_counts: int32 [4, 32, 32], P(None, ('lon', 'lat')), may hold values from 1 to 4, as said below
- innovations: float32 [4, 32, 32, 4, 128], P(None, ('lon', 'lat')), may hold values from -6 to 6
- error_weight: float32 [4, 32, 32, 4, 128], P(None, ('lon', 'lat')), may hold values from 0.3 to 3
- weighting: float32 [274, 128], replicated, may hold values from -0.375 to 0.375
Outputs:
- solution: float32 [2, 137, 32, 512], P(None, None, 'lon', 'lat')
- residual: float32 [2, 137, 32, 512], P(None, None, 'lon', 'lat')
The draws below stay inside these ranges and needn't reach their ends.
Inputs may be any that keep to these rules, and one draw needn't show every extreme that they name: `slot_column_cells`: A cell of the sending device's block, numbered longitude-major over its 4 x 128 cells; only slots below the matching count are read. `column_counts`: at every timestep some owner receives 4 live slots from every sending device.
All inputs are finite; a program needn't handle non-finite values.
Results may differ from the reference program's by a relative error of at most 0.00016.
Values sent between devices are 32-bit elements; how exact they have to be, the bound alone decides.
A program may use at most 128 MiB of HBM per device.

```python
import math
import jax
import jax.numpy as jnp
from jax import lax

LEV = 137
CHAN = 128
NT = 4
ITERS = 2
CAP = 4
LONC = 4
LATC = 128
NLON = 32
NLAT = 512
CELLS = 512
N_LAT = 4
DEVICES = 32


def draw_column_counts(key, part):
    level_key = jax.random.fold_in(key, 11)
    count_key = jax.random.fold_in(key, 12)
    owner_key = jax.random.fold_in(key, 13)
    ceiling = jnp.minimum(jnp.power(2, jax.random.randint(level_key, (1, 1, DEVICES), 1, 3)), CAP)
    counts = jax.random.randint(count_key, (NT, DEVICES, DEVICES), ceiling // 2, ceiling + 1)
    crowded = jax.random.randint(owner_key, (NT, 1, 1), 0, DEVICES)
    owner_index = lax.broadcasted_iota(jnp.int32, (NT, DEVICES, DEVICES), 2)
    return jnp.where(owner_index == crowded, CAP, counts).astype(jnp.int32)


def set_ends(values, own_key, low, top_value):
    longest = values.shape.index(max(values.shape))
    spots = []
    for shift in (0, 1):
        where = [jax.random.randint(jax.random.fold_in(own_key, axis), (), 0, length) for axis, length in enumerate(values.shape)]
        where[longest] = (where[longest] + shift) % values.shape[longest]
        spots.append(tuple(where))
    return values.at[spots[0]].set(low).at[spots[1]].set(top_value)


def shard_levels(key, dims, shards, low, high):
    level = 1.0
    for dim, shards_of in shards:
        draws = jax.random.uniform(jax.random.fold_in(jax.random.fold_in(key, 6), dim), (shards_of,), jnp.float32, low / len(shards), high / len(shards))
        level = level * jnp.repeat(jnp.exp(draws), dims[dim] // shards_of).reshape((-1,) + (1,) * (len(dims) - 1 - dim))
    return level


def gaussian(stream_key, dims, deviation, reach, split=(), dtype=jnp.bfloat16):
    factor_of = shard_levels(stream_key, dims, split, -0.22, 0.18) if split else 1.0
    array = jax.random.normal(stream_key, dims, jnp.float32) * deviation * factor_of
    return jnp.minimum(jnp.maximum(array, -reach), reach).astype(dtype)


def setup_inputs(seed: int = 0) -> dict:
    streams_of = jax.random.split(jax.random.key(seed), 7)
    courant = jnp.clip(jax.random.uniform(streams_of[0], (NT, 2, LEV, NLON, NLAT), jnp.float32, -0.45, 0.45) * shard_levels(streams_of[0], (NT, 2, LEV, NLON, NLAT), ((3, 8), (4, 4)), -0.4, 0.0), -0.45, 0.45)
    slot_column_cells = set_ends(jax.random.randint(streams_of[1], (NT, DEVICES, DEVICES, CAP), 0, CELLS), jax.random.fold_in(streams_of[1], 1), 0, CELLS - 1).astype(jnp.int32)
    column_counts = draw_column_counts(jax.random.fold_in(streams_of[6], 71), 0)
    innovations = gaussian(streams_of[3], (NT, DEVICES, DEVICES, CAP, CHAN), 1.0, 6.0, ((1, 32),), jnp.float32)
    error_weight = jnp.clip(jnp.exp(math.log(3.0) - 2.3025851 * jax.random.uniform(streams_of[4], (NT, DEVICES, DEVICES, CAP, CHAN), jnp.float32) ** shard_levels(streams_of[4], (NT, DEVICES, DEVICES, CAP, CHAN), ((1, 32),), -0.2, 0.2)), 0.3, 3.0)
    weighting = gaussian(streams_of[5], (2 * LEV, CHAN), (2 * LEV) ** -0.5, 0.375, (), jnp.float32)
    return {"courant": courant, "slot_column_cells": slot_column_cells, "column_counts": column_counts, "innovations": innovations, "error_weight": error_weight, "weighting": weighting}


def advance(states, east_courant, north_courant):
    from_west = jnp.roll(states, 1, axis=2)
    from_east = jnp.roll(states, -1, axis=2)
    padded = jnp.pad(states, ((0, 0), (0, 0), (0, 0), (1, 1)))
    result = (1.0 - jnp.abs(east_courant) - jnp.abs(north_courant)) * states
    result = result + jnp.maximum(east_courant, 0.0) * from_west
    result = result + jnp.maximum(-east_courant, 0.0) * from_east
    result = result + jnp.maximum(north_courant, 0.0) * padded[:, :, :, :-2]
    result = result + jnp.maximum(-north_courant, 0.0) * padded[:, :, :, 2:]
    return result


def retreat(states, east_courant, north_courant):
    widths = ((0, 0), (0, 0), (0, 0), (1, 1))
    eastward = jnp.maximum(east_courant, 0.0) * states
    westward = jnp.maximum(-east_courant, 0.0) * states
    northward = jnp.pad(jnp.maximum(north_courant, 0.0) * states, widths)
    southward = jnp.pad(jnp.maximum(-north_courant, 0.0) * states, widths)
    result = (1.0 - jnp.abs(east_courant) - jnp.abs(north_courant)) * states
    result = result + jnp.roll(eastward, -1, axis=2)
    result = result + jnp.roll(westward, 1, axis=2)
    result = result + northward[:, :, :, 2:]
    result = result + southward[:, :, :, :-2]
    return result


def reference(courant, slot_column_cells, column_counts, innovations, error_weight, weighting):
    column_depth = 2 * LEV
    cell_total = NLON * NLAT
    highest = lax.Precision.HIGHEST
    sources = lax.broadcasted_iota(jnp.int32, (NT, DEVICES, DEVICES, CAP), 1)
    longitude = (sources // N_LAT) * LONC + slot_column_cells // LATC
    latitude = (sources % N_LAT) * LATC + slot_column_cells % LATC
    flat_index = (longitude * NLAT + latitude).astype(jnp.int32)
    slot_position = lax.broadcasted_iota(jnp.int32, (NT, DEVICES, DEVICES, CAP), 3)
    active = (slot_position < column_counts[:, :, :, None]).astype(jnp.float32)

    def observe(states, time_moment):
        columns = states.reshape(column_depth, cell_total)[:, flat_index[time_moment]]
        columns = columns * active[time_moment]
        return jnp.einsum("kgoc,kh->ogch", columns, weighting, precision=highest)

    def deposit(weighted, time_moment):
        gradient = jnp.einsum("ogch,kh->kgoc", weighted, weighting, precision=highest) * active[time_moment]
        total = jnp.zeros((column_depth, cell_total), jnp.float32)
        total = total.at[:, flat_index[time_moment].reshape(-1)].add(gradient.reshape(column_depth, -1))
        return total.reshape(2, LEV, NLON, NLAT)

    def tangent(states):
        payloads = []
        for time_moment in range(NT):
            states = advance(states, courant[time_moment, 0], courant[time_moment, 1])
            payloads.append(error_weight[time_moment] * observe(states, time_moment))
        return payloads

    def adjoint_sweep(payloads):
        sensitivity = jnp.zeros((2, LEV, NLON, NLAT), jnp.float32)
        for time_moment in reversed(range(NT)):
            sensitivity = sensitivity + deposit(payloads[time_moment], time_moment)
            sensitivity = retreat(sensitivity, courant[time_moment, 0], courant[time_moment, 1])
        return sensitivity

    def hessian(direction):
        return direction + adjoint_sweep(tangent(direction))

    weighted_all = error_weight * innovations
    right_hand_side = adjoint_sweep([weighted_all[time_moment] for time_moment in range(NT)])
    solution = jnp.zeros((2, LEV, NLON, NLAT), jnp.float32)
    residual = right_hand_side
    direction = right_hand_side
    residual_norm = jnp.sum(residual * residual)
    for iteration in range(ITERS):
        hessian_image = hessian(direction)
        step_length = residual_norm / jnp.sum(direction * hessian_image)
        solution = solution + step_length * direction
        residual = residual - step_length * hessian_image
        if iteration + 1 < ITERS:
            updated = jnp.sum(residual * residual)
            direction = residual + (updated / residual_norm) * direction
            residual_norm = updated
    return solution, residual
```

```python
import functools

import jax
import jax.numpy as jnp
from jax import lax
from jax.experimental import pallas as pl
from jax.experimental.pallas import tpu as pltpu
from jax.sharding import PartitionSpec as P

ITERS = 2
CHUNKS = 4
TILE = 24
MESH = pl.DeviceIdType.MESH
F32 = jnp.float32
BF16 = jnp.bfloat16


def split(value):
    high = value.astype(BF16)
    return high, (value - high.astype(F32)).astype(BF16)


def dot(a, b):
    return jnp.dot(a, b, preferred_element_type=F32)


def dot_nt(a, b):
    return lax.dot_general(a, b, (((1,), (1,)), ((), ())), preferred_element_type=F32)


def kernel(
    lon_n, lat_n, valid,
    courant, cells, scale, target, up_w, down_w,
    x_out, r_out,
    p, s, dep, y_acc, v_dep, onehot, seen,
    snd, rcv, part1, part2, sums1, sums2,
    ssem, rsem, s1, r1, s2, r2,
):
    times, _, slab, levels, band = courant.shape
    chan = up_w.shape[1]
    rows_h = 2 * levels // CHUNKS
    per_var = levels // rows_h
    a = lax.axis_index("lon")
    b = lax.axis_index("lat")
    peers = (
        (lax.rem(a + lon_n - 1, lon_n), b),
        (lax.rem(a + 1, lon_n), b),
        (a, lax.rem(b + lat_n - 1, lat_n)),
        (a, lax.rem(b + 1, lat_n)),
    )

    for par in range(2):
        for d in range(4):
            for var in range(2):
                tail = slice(var * levels + valid // 8 * 8, (var + 1) * levels)
                rcv[par, d, tail, :] = jnp.zeros((levels - valid // 8 * 8, band), F32)
    barrier = pltpu.get_barrier_semaphore()
    for off in range(1, lon_n):
        pl.semaphore_signal(barrier, inc=1, device_id=(lax.rem(a + off, lon_n), b), device_id_type=MESH)
    for off in range(1, lat_n):
        pl.semaphore_signal(barrier, inc=1, device_id=(a, lax.rem(b + off, lat_n)), device_id_type=MESH)

    lane = lax.broadcasted_iota(jnp.int32, (TILE, band), 1)
    has_south = (b > 0).astype(F32)
    has_north = (b < lat_n - 1).astype(F32)
    cols = [slice(i * band, (i + 1) * band) for i in range(slab)]

    def copies(par, h):
        span = pl.ds(h * rows_h, min(rows_h, valid - (h % per_var) * rows_h))
        return [
            pltpu.make_async_remote_copy(
                src_ref=snd.at[par, d, span],
                dst_ref=rcv.at[par, d, span],
                send_sem=ssem.at[par, h, d],
                recv_sem=rsem.at[par, h, d],
                device_id=peers[d],
                device_id_type=MESH,
            )
            for d in range(4)
        ]

    def start(par, h):
        for copy in copies(par, h):
            copy.start()

    def wait(par, h):
        for copy in copies(par, h):
            copy.wait()

    def tiles(h, body, carry=None):
        for n in range(rows_h // TILE):
            row = pl.ds(h * rows_h + n * TILE, TILE)
            crow = pl.ds((h % per_var) * rows_h + n * TILE, TILE)
            carry = body(row, crow, carry)
        return carry

    def winds(t, crow):
        return (
            [courant[t, 0, i, crow, :] for i in range(slab)],
            [courant[t, 1, i, crow, :] for i in range(slab)],
        )

    def load(ref, row):
        return [ref[row, c] for c in cols]

    def store(ref, row, values):
        for c, value in zip(cols, values):
            ref[row, c] = value

    def turn(value, shift):
        shift = shift % band
        return value if shift == 0 else pltpu.roll(value, shift, 1)

    def halos(par, row):
        from_south = rcv[par, 3, row, :] * has_south
        from_north = rcv[par, 2, row, :] * has_north
        return rcv[par, 1, row, :], rcv[par, 0, row, :], from_south, from_north

    def shifted(value, halo, i, up):
        if up:
            return jnp.where(lane == 0, turn(halo, -i), turn(value, 1))
        return jnp.where(lane == band - 1, turn(halo, slab - 1 - i), turn(value, -1))

    def advance(t, row, crow, par):
        u, v = winds(t, crow)
        x = load(s, row)
        west, east, south, north = halos(par, row)
        full = [west] + x + [east]
        outs = []
        for i in range(slab):
            out = (1.0 - jnp.abs(u[i]) - jnp.abs(v[i])) * x[i]
            out += jnp.maximum(u[i], 0.0) * full[i]
            out += jnp.maximum(-u[i], 0.0) * full[i + 2]
            out += jnp.maximum(v[i], 0.0) * shifted(x[i], south, i, True)
            out += jnp.maximum(-v[i], 0.0) * shifted(x[i], north, i, False)
            outs.append(out)
        return outs

    def retreat(t, row, crow, par):
        u, v = winds(t, crow)
        y = load(s, row)
        west, east, south, north = halos(par, row)
        plus = [jnp.maximum(u[i], 0.0) * y[i] for i in range(slab)] + [east]
        minus = [west] + [jnp.maximum(-u[i], 0.0) * y[i] for i in range(slab)]
        outs = []
        for i in range(slab):
            out = (1.0 - jnp.abs(u[i]) - jnp.abs(v[i])) * y[i]
            out += plus[i + 1] + minus[i]
            out += shifted(jnp.maximum(v[i], 0.0) * y[i], north, i, False)
            out += shifted(jnp.maximum(-v[i], 0.0) * y[i], south, i, True)
            outs.append(out)
        return outs

    def put_edges(par, row, west, east, southward, northward):
        snd[par, 0, row, :] = west
        snd[par, 1, row, :] = east
        low = jnp.zeros((TILE, band), F32)
        high = low
        for i in range(slab):
            low = jnp.where(lane == band - slab + i, turn(southward[i], band - slab + i), low)
            high = jnp.where(lane == i, turn(northward[i], i + 1), high)
        snd[par, 2, row, :] = low
        snd[par, 3, row, :] = high

    def put_state(par, row, x):
        put_edges(par, row, x[0], x[-1], x, x)

    def put_products(par, t, row, crow, y):
        u, v = winds(t, crow)
        put_edges(
            par, row,
            jnp.maximum(u[0], 0.0) * y[0],
            jnp.maximum(-u[-1], 0.0) * y[-1],
            [jnp.maximum(v[i], 0.0) * y[i] for i in range(slab)],
            [jnp.maximum(-v[i], 0.0) * y[i] for i in range(slab)],
        )

    def project(var):
        high, low = split(s[var * levels : (var + 1) * levels, :])
        y = dot(up_w[var], jnp.concatenate([high, high, low], axis=0))
        if var == 0:
            y_acc[...] = y
        else:
            y_acc[...] += y

    def scatter(t, weigh):
        pair = jnp.concatenate(split(weigh(t)), axis=0)
        both = dot_nt(pair, onehot[t])
        high, low = split(both[:chan] + both[chan:])
        v_dep[:chan, :] = high
        v_dep[chan : 2 * chan, :] = high
        v_dep[2 * chan :, :] = low

    def observe(k, t):
        pair = jnp.concatenate(split(y_acc[...]), axis=0)
        both = dot(pair, onehot[t])
        seen[k, t] = both[:chan] + both[chan:]

    def deposit(var, into):
        span = slice(var * levels, (var + 1) * levels)
        into[span, :] = dot(down_w[span, :], v_dep[...])

    def adjoint(weigh, finish, carry, pass_on, slot=None, partials=None):
        scatter(times - 1, weigh)
        for var in range(2):
            deposit(var, s)
            for h in range(var * per_var, (var + 1) * per_var):
                def enter(row, crow, none):
                    put_products(0, times - 1, row, crow, load(s, row))

                tiles(h, enter)
                start(0, h)
        if slot is not None:
            first_leg(slot, *partials())

        def step(n, none):
            t = times - 1 - n
            par = lax.rem(n, 2)
            scatter(t - 1, weigh)
            for var in range(2):
                deposit(var, dep)
            if slot is not None:
                @pl.when(n == 1)
                def _():
                    second_leg(slot)

            for h in range(CHUNKS):
                wait(par, h)

                def back(row, crow, none):
                    y = [v + d for v, d in zip(retreat(t, row, crow, par), load(dep, row))]
                    store(s, row, y)
                    put_products(1 - par, t - 1, row, crow, y)

                tiles(h, back)
                start(1 - par, h)
            return none

        lax.fori_loop(0, times - 1, step, 0)
        if slot is not None:
            finish = finish(*totals(slot))
        par = (times - 1) % 2
        for h in range(CHUNKS):
            wait(par, h)

            def last(row, crow, carry):
                return finish(row, retreat(0, row, crow, par), carry)

            carry = tiles(h, last, carry)
            if pass_on:
                start(0, h)
        return carry

    def tangent(k, slot=None):
        def step(t, none):
            par = lax.rem(t, 2)
            if slot is not None:
                @pl.when(t == 1)
                def _():
                    second_leg(slot)

            for h in range(CHUNKS):
                wait(par, h)

                def onward(row, crow, none):
                    x = advance(t, row, crow, par)
                    store(s, row, x)
                    put_state(1 - par, row, x)

                tiles(h, onward)
                start(1 - par, h)
                if (h + 1) % per_var == 0:
                    project(h // per_var)
            observe(k, t)
            return none

        lax.fori_loop(0, times - 1, step, 0)
        par = (times - 1) % 2
        for h in range(CHUNKS):
            wait(par, h)

            def last(row, crow, none):
                store(s, row, advance(times - 1, row, crow, par))

            tiles(h, last)
            if (h + 1) % per_var == 0:
                project(h // per_var)
        observe(k, times - 1)

    def legs(k, axis):
        count, me, source, sums, send, receive = (
            (lon_n, a, part1, sums1, s1, r1),
            (lat_n, b, part2, sums2, s2, r2),
        )[axis]
        moves = []
        for off in range(1, count):
            other = lax.rem(me + off, count)
            moves.append(
                pltpu.make_async_remote_copy(
                    src_ref=source.at[k],
                    dst_ref=sums.at[k, me],
                    send_sem=send.at[k, off - 1],
                    recv_sem=receive.at[k, off - 1],
                    device_id=(other, b) if axis == 0 else (a, other),
                    device_id_type=MESH,
                )
            )
        return moves

    def launch(k, axis, tile):
        source, sums, me = ((part1, sums1, a), (part2, sums2, b))[axis]
        source[k] = tile
        sums[k, me] = tile
        for move in legs(k, axis):
            move.start()

    def land(k, axis):
        for move in legs(k, axis):
            move.wait()
        sums, count = ((sums1, lon_n), (sums2, lat_n))[axis]
        total = sums[k, 0]
        for j in range(1, count):
            total = total + sums[k, j]
        return total

    def first_leg(k, first, second):
        launch(k, 0, jnp.concatenate([first, second], axis=0))

    def second_leg(k):
        launch(k, 1, land(k, 0))

    def totals(k):
        tile = land(k, 1)
        return [jnp.sum(tile[8 * n : 8 * n + 8], keepdims=True) for n in range(2)]

    def fold(value):
        return value.reshape(TILE // 8, 8, band).sum(0)

    slots = cells.shape[-1]
    place = lax.broadcasted_iota(jnp.int32, (slab * band, slots), 0)
    for t in range(times):
        here = jnp.broadcast_to(cells[t], (slab * band, slots))
        onehot[t] = jnp.where(here == place, 1.0, 0.0).astype(BF16)
    pl.semaphore_wait(barrier, lon_n + lat_n - 2)

    zero = jnp.zeros((8, band), F32)

    def begin(row, values, acc):
        put_state(0, row, values)
        for value in values:
            acc = acc + fold(value * value)
        store(s, row, values)
        store(p, row, values)
        return acc

    def norm(value):
        value = value.reshape(-1, 8, value.shape[-1]).sum(0)
        width = value.shape[-1]
        return sum(value[:, i : i + band] for i in range(0, width, band))

    def weigh_first(t):
        return scale[t] * seen[0, t]

    acc = adjoint(lambda t: target[t], begin, zero, True)
    tangent(0)
    scalars = []

    def energy_first():
        total = zero
        for t in range(times):
            total = total + norm(weigh_first(t) * seen[0, t])
        return acc, total

    def imager(rho, energy):
        scalars.extend([rho, energy])

        def image(row, values, qq):
            outs = []
            for d, value in zip(load(p, row), values):
                q = d + value
                outs.append(q)
                qq = qq + fold(q * q)
            put_state(0, row, outs)
            store(s, row, outs)
            store(r_out, row, outs)
            return qq

        return image

    qq = adjoint(weigh_first, imager, zero, True, 0, energy_first)
    first_leg(1, qq, zero)
    tangent(1, 1)
    rho, energy = scalars
    qq = totals(1)[0]
    pq = rho + energy
    alpha = rho / pq
    rho_new = rho - 2.0 * alpha * pq + alpha * alpha * qq
    beta = rho_new / rho
    grown = 1.0 + beta
    square = rho_new + beta * beta * rho

    def seen_next(t):
        return grown * seen[0, t] - alpha * seen[1, t]

    def weigh_next(t):
        return scale[t] * seen_next(t)

    def energy_next():
        total = zero
        for t in range(times):
            y = seen_next(t)
            total = total + norm(scale[t] * y * y)
        return total, zero

    def closer(energy, none):
        step = rho_new / (square + energy)

        def close(row, values, carry):
            first = load(p, row)
            image = load(r_out, row)
            d = [grown * v - alpha * q for v, q in zip(first, image)]
            store(x_out, row, [alpha * v + step * w for v, w in zip(first, d)])
            residual = [v - alpha * q for v, q in zip(first, image)]
            store(r_out, row, [v - step * (w + z) for v, w, z in zip(residual, d, values)])
            return carry

        return close

    adjoint(weigh_next, closer, 0, False, 2, energy_next)


def pair_of(value):
    high = lax.reduce_precision(value, 8, 7)
    return high, lax.reduce_precision(value - high, 8, 7)


def body(courant, slot_column_cells, column_counts, innovations, error_weight, weighting):
    times, _, levels, slab, band = courant.shape
    owners, cap = slot_column_cells.shape[2:]
    chan = weighting.shape[1]
    slots = owners * cap
    lon_n, lat_n = lax.axis_size("lon"), lax.axis_size("lat")
    deep = -(-levels // 48) * 48

    field = jnp.pad(courant.transpose(0, 1, 3, 2, 4), ((0, 0),) * 3 + ((0, deep - levels), (0, 0)))
    weights = jnp.pad(weighting.reshape(2, levels, chan), ((0, 0), (0, deep - levels), (0, 0)))
    high, low = pair_of(weights)
    down_w = jnp.concatenate([high, low, high], axis=2).reshape(2 * deep, 3 * chan).astype(BF16)
    up_w = jnp.concatenate([high, low, high], axis=1).transpose(0, 2, 1).astype(BF16)
    here = error_weight[:, 0]
    both = jnp.stack([here, here * innovations[:, 0]]).transpose(2, 0, 1, 3, 4)
    both = lax.all_to_all(both, ("lon", "lat"), split_axis=0, concat_axis=0, tiled=True)
    position = lax.broadcasted_iota(jnp.int32, (times, owners, cap), 2)
    live = (position < column_counts[:, 0][:, :, None]).astype(F32).reshape(times, 1, slots)
    both = both.transpose(1, 2, 4, 0, 3).reshape(2, times, chan, slots) * live
    cells = slot_column_cells[:, 0].reshape(times, 1, slots)

    state = (2 * deep, slab * band)
    vmem = pl.BlockSpec(memory_space=pltpu.VMEM)
    sums = 3
    x, r = pl.pallas_call(
        functools.partial(kernel, lon_n, lat_n, levels),
        out_shape=[jax.ShapeDtypeStruct(state, F32)] * 2,
        in_specs=[vmem] * 6,
        out_specs=[vmem] * 2,
        scratch_shapes=[
            pltpu.VMEM(state, F32),
            pltpu.VMEM(state, F32),
            pltpu.VMEM(state, F32),
            pltpu.VMEM((chan, slab * band), F32),
            pltpu.VMEM((3 * chan, slab * band), BF16),
            pltpu.VMEM((times, slab * band, slots), BF16),
            pltpu.VMEM((ITERS, times, chan, slots), F32),
            pltpu.VMEM((2, 4, 2 * deep, band), F32),
            pltpu.VMEM((2, 4, 2 * deep, band), F32),
            pltpu.VMEM((sums, 16, band), F32),
            pltpu.VMEM((sums, 16, band), F32),
            pltpu.VMEM((sums, lon_n, 16, band), F32),
            pltpu.VMEM((sums, lat_n, 16, band), F32),
            pltpu.SemaphoreType.DMA((2, CHUNKS, 4)),
            pltpu.SemaphoreType.DMA((2, CHUNKS, 4)),
            pltpu.SemaphoreType.DMA((sums, lon_n - 1)),
            pltpu.SemaphoreType.DMA((sums, lon_n - 1)),
            pltpu.SemaphoreType.DMA((sums, lat_n - 1)),
            pltpu.SemaphoreType.DMA((sums, lat_n - 1)),
        ],
        compiler_params=pltpu.CompilerParams(collective_id=0, has_side_effects=True, vmem_limit_bytes=48 * 2**20),
    )(field, cells, both[0], both[1], up_w, down_w)

    def back(state):
        return state.reshape(2, deep, slab, band)[:, :levels]

    return back(x), back(r)


def solution(mesh):
    owned = ("lon", "lat")
    in_specs = (
        P(None, None, None, "lon", "lat"),
        P(None, owned, None, None),
        P(None, owned, None),
        P(None, owned, None, None, None),
        P(None, owned, None, None, None),
        P(),
    )
    out_specs = (P(None, None, "lon", "lat"), P(None, None, "lon", "lat"))
    return jax.shard_map(body, mesh=mesh, in_specs=in_specs, out_specs=out_specs, check_vma=False)
```

```python
import functools

import jax
import jax.numpy as jnp
from jax import lax
from jax.experimental import pallas as pl
from jax.experimental.pallas import tpu as pltpu
from jax.sharding import PartitionSpec as P

ITERS = 2
CHUNKS = 4
TILE = 24
MESH = pl.DeviceIdType.MESH
F32 = jnp.float32
BF16 = jnp.bfloat16


def split(value):
    high = value.astype(BF16)
    return high, (value - high.astype(F32)).astype(BF16)


def dot(a, b):
    return jnp.dot(a, b, preferred_element_type=F32)


def dot_nt(a, b):
    return lax.dot_general(a, b, (((1,), (1,)), ((), ())), preferred_element_type=F32)


def kernel(
    lon_n, lat_n, valid,
    raw, cells, live, innovations, weights, up_w, down_w,
    x_out, r_out,
    courant, scale, target, sent, came, heavy,
    p, s, keep, dep, y_acc, v_dep, onehot, seen,
    snd, rcv, part1, part2, sums1, sums2,
    ssem, rsem, s1, r1, s2, r2, asem, bsem,
):
    times, _, slab, levels, band = courant.shape
    count, cap = sent.shape[1:3]
    chan = up_w.shape[1]
    rows_h = 2 * levels // CHUNKS
    per_var = levels // rows_h
    a = lax.axis_index("lon")
    b = lax.axis_index("lat")
    peers = (
        (lax.rem(a + lon_n - 1, lon_n), b),
        (lax.rem(a + 1, lon_n), b),
        (a, lax.rem(b + lat_n - 1, lat_n)),
        (a, lax.rem(b + 1, lat_n)),
    )

    for par in range(2):
        for d in range(4):
            for var in range(2):
                tail = slice(var * levels + valid // 8 * 8, (var + 1) * levels)
                rcv[par, d, tail, :] = jnp.zeros((levels - valid // 8 * 8, band), F32)
    me = a * lat_n + b

    def place_of(off):
        other = lax.rem(me + off, count)
        return other, (other // lat_n, lax.rem(other, lat_n))

    barrier = pltpu.get_barrier_semaphore()

    def greet(off, none):
        pl.semaphore_signal(barrier, inc=1, device_id=place_of(off)[1], device_id_type=MESH)
        return none

    lax.fori_loop(1, count, greet, 0)

    lane = lax.broadcasted_iota(jnp.int32, (TILE, band), 1)
    has_south = (b > 0).astype(F32)
    has_north = (b < lat_n - 1).astype(F32)
    cols = [slice(i * band, (i + 1) * band) for i in range(slab)]

    def copies(par, h):
        span = pl.ds(h * rows_h, min(rows_h, valid - (h % per_var) * rows_h))
        return [
            pltpu.make_async_remote_copy(
                src_ref=snd.at[par, d, span],
                dst_ref=rcv.at[par, d, span],
                send_sem=ssem.at[par, h, d],
                recv_sem=rsem.at[par, h, d],
                device_id=peers[d],
                device_id_type=MESH,
            )
            for d in range(4)
        ]

    def start(par, h):
        for copy in copies(par, h):
            copy.start()

    def wait(par, h):
        for copy in copies(par, h):
            copy.wait()

    def tiles(h, body, carry=None):
        for n in range(rows_h // TILE):
            row = pl.ds(h * rows_h + n * TILE, TILE)
            crow = pl.ds((h % per_var) * rows_h + n * TILE, TILE)
            carry = body(row, crow, carry)
        return carry

    def winds(t, crow):
        return (
            [courant[t, 0, i, crow, :] for i in range(slab)],
            [courant[t, 1, i, crow, :] for i in range(slab)],
        )

    def load(ref, row):
        return [ref[row, c] for c in cols]

    def store(ref, row, values):
        for c, value in zip(cols, values):
            ref[row, c] = value

    def turn(value, shift):
        shift = shift % band
        return value if shift == 0 else pltpu.roll(value, shift, 1)

    def halos(par, row):
        from_south = rcv[par, 3, row, :] * has_south
        from_north = rcv[par, 2, row, :] * has_north
        return rcv[par, 1, row, :], rcv[par, 0, row, :], from_south, from_north

    def shifted(value, halo, i, up):
        if up:
            return jnp.where(lane == 0, turn(halo, -i), turn(value, 1))
        return jnp.where(lane == band - 1, turn(halo, slab - 1 - i), turn(value, -1))

    def advance(t, row, crow, par):
        u, v = winds(t, crow)
        x = load(s, row)
        west, east, south, north = halos(par, row)
        full = [west] + x + [east]
        outs = []
        for i in range(slab):
            out = (1.0 - jnp.abs(u[i]) - jnp.abs(v[i])) * x[i]
            out += jnp.maximum(u[i], 0.0) * full[i]
            out += jnp.maximum(-u[i], 0.0) * full[i + 2]
            out += jnp.maximum(v[i], 0.0) * shifted(x[i], south, i, True)
            out += jnp.maximum(-v[i], 0.0) * shifted(x[i], north, i, False)
            outs.append(out)
        return outs

    def retreat(t, row, crow, par):
        u, v = winds(t, crow)
        y = load(s, row)
        west, east, south, north = halos(par, row)
        plus = [jnp.maximum(u[i], 0.0) * y[i] for i in range(slab)] + [east]
        minus = [west] + [jnp.maximum(-u[i], 0.0) * y[i] for i in range(slab)]
        outs = []
        for i in range(slab):
            out = (1.0 - jnp.abs(u[i]) - jnp.abs(v[i])) * y[i]
            out += plus[i + 1] + minus[i]
            out += shifted(jnp.maximum(v[i], 0.0) * y[i], north, i, False)
            out += shifted(jnp.maximum(-v[i], 0.0) * y[i], south, i, True)
            outs.append(out)
        return outs

    def put_edges(par, row, west, east, southward, northward):
        snd[par, 0, row, :] = west
        snd[par, 1, row, :] = east
        low = jnp.zeros((TILE, band), F32)
        high = low
        for i in range(slab):
            low = jnp.where(lane == band - slab + i, turn(southward[i], band - slab + i), low)
            high = jnp.where(lane == i, turn(northward[i], i + 1), high)
        snd[par, 2, row, :] = low
        snd[par, 3, row, :] = high

    def put_state(par, row, x):
        put_edges(par, row, x[0], x[-1], x, x)

    def put_products(par, t, row, crow, y):
        u, v = winds(t, crow)
        put_edges(
            par, row,
            jnp.maximum(u[0], 0.0) * y[0],
            jnp.maximum(-u[-1], 0.0) * y[-1],
            [jnp.maximum(v[i], 0.0) * y[i] for i in range(slab)],
            [jnp.maximum(-v[i], 0.0) * y[i] for i in range(slab)],
        )

    def project(var):
        high, low = split(s[var * levels : (var + 1) * levels, :])
        y = dot(up_w[var], jnp.concatenate([high, high, low], axis=0))
        if var == 0:
            y_acc[...] = y
        else:
            y_acc[...] += y

    def scatter(t, weigh):
        pair = jnp.concatenate(split(weigh(t)), axis=0)
        both = dot_nt(pair, onehot[t])
        high, low = split(both[:chan] + both[chan:])
        v_dep[:chan, :] = high
        v_dep[chan : 2 * chan, :] = high
        v_dep[2 * chan :, :] = low

    def observe(k, t):
        pair = jnp.concatenate(split(y_acc[...]), axis=0)
        both = dot(pair, onehot[t])
        seen[k, t] = both[:chan] + both[chan:]

    def deposit(var, into):
        span = slice(var * levels, (var + 1) * levels)
        into[span, :] = dot(down_w[span, :], v_dep[...])

    def adjoint(weigh, finish, carry, pass_on, slot=None, partials=None):
        scatter(times - 1, weigh)
        for var in range(2):
            deposit(var, s)
            for h in range(var * per_var, (var + 1) * per_var):
                def enter(row, crow, none):
                    put_products(0, times - 1, row, crow, load(s, row))

                tiles(h, enter)
                start(0, h)
        if slot is not None:
            first_leg(slot, *partials())

        def step(n, none):
            t = times - 1 - n
            par = lax.rem(n, 2)
            scatter(t - 1, weigh)
            for var in range(2):
                deposit(var, dep)
            if slot is not None:
                @pl.when(n == 1)
                def _():
                    second_leg(slot)

            for h in range(CHUNKS):
                wait(par, h)

                def back(row, crow, none):
                    y = [v + d for v, d in zip(retreat(t, row, crow, par), load(dep, row))]
                    store(s, row, y)
                    put_products(1 - par, t - 1, row, crow, y)

                tiles(h, back)
                start(1 - par, h)
            return none

        lax.fori_loop(0, times - 1, step, 0)
        if slot is not None:
            finish = finish(*totals(slot))
        par = (times - 1) % 2
        for h in range(CHUNKS):
            wait(par, h)

            def last(row, crow, carry):
                return finish(row, retreat(0, row, crow, par), carry)

            carry = tiles(h, last, carry)
            if pass_on:
                start(0, h)
        return carry

    def tangent(k, slot=None):
        def step(t, none):
            par = lax.rem(t, 2)
            if slot is not None:
                @pl.when(t == 1)
                def _():
                    second_leg(slot)

            for h in range(CHUNKS):
                wait(par, h)

                def onward(row, crow, none):
                    x = advance(t, row, crow, par)
                    store(s, row, x)
                    put_state(1 - par, row, x)

                tiles(h, onward)
                start(1 - par, h)
                if (h + 1) % per_var == 0:
                    project(h // per_var)
            observe(k, t)
            return none

        lax.fori_loop(0, times - 1, step, 0)
        par = (times - 1) % 2
        for h in range(CHUNKS):
            wait(par, h)

            def last(row, crow, none):
                store(s, row, advance(times - 1, row, crow, par))

            tiles(h, last)
            if (h + 1) % per_var == 0:
                project(h // per_var)
        observe(k, times - 1)

    def legs(k, axis):
        count, me, source, sums, send, receive = (
            (lon_n, a, part1, sums1, s1, r1),
            (lat_n, b, part2, sums2, s2, r2),
        )[axis]
        moves = []
        for off in range(1, count):
            other = lax.rem(me + off, count)
            moves.append(
                pltpu.make_async_remote_copy(
                    src_ref=source.at[k],
                    dst_ref=sums.at[k, me],
                    send_sem=send.at[k, off - 1],
                    recv_sem=receive.at[k, off - 1],
                    device_id=(other, b) if axis == 0 else (a, other),
                    device_id_type=MESH,
                )
            )
        return moves

    def launch(k, axis, tile):
        source, sums, me = ((part1, sums1, a), (part2, sums2, b))[axis]
        source[k] = tile
        sums[k, me] = tile
        for move in legs(k, axis):
            move.start()

    def land(k, axis):
        for move in legs(k, axis):
            move.wait()
        sums, count = ((sums1, lon_n), (sums2, lat_n))[axis]
        total = sums[k, 0]
        for j in range(1, count):
            total = total + sums[k, j]
        return total

    def first_leg(k, first, second):
        launch(k, 0, jnp.concatenate([first, second], axis=0))

    def second_leg(k):
        launch(k, 1, land(k, 0))

    def totals(k):
        tile = land(k, 1)
        return [jnp.sum(tile[8 * n : 8 * n + 8], keepdims=True) for n in range(2)]

    def parcel(which, source, landing, off):
        other, device = place_of(off)
        return pltpu.make_async_remote_copy(
            src_ref=source.at[:, other],
            dst_ref=landing.at[:, me],
            send_sem=asem.at[which, off - 1],
            recv_sem=bsem.at[which, off - 1],
            device_id=device,
            device_id_type=MESH,
        )

    def post(which, source, landing):
        landing[:, me] = source[:, me]

        def one(off, none):
            parcel(which, source, landing, off).start()
            return none

        lax.fori_loop(1, count, one, 0)

    def collect(which, source, landing, into):
        def one(off, none):
            parcel(which, source, landing, off).wait()
            return none

        lax.fori_loop(1, count, one, 0)
        for t in range(times):
            rows = jnp.concatenate([landing[t, :, c, :] for c in range(cap)], axis=0)
            into[t] = rows.T * live[t]

    def fold(value):
        return value.reshape(TILE // 8, 8, band).sum(0)

    slots = cells.shape[-1]
    place = lax.broadcasted_iota(jnp.int32, (slab * band, slots), 0)
    for t in range(times):
        here = jnp.broadcast_to(cells[t], (slab * band, slots))
        onehot[t] = jnp.where(here == place, 1.0, 0.0).astype(BF16)
    for t in range(times):
        sent[t] = weights[t] * innovations[t]
    pl.semaphore_wait(barrier, count - 1)
    post(0, sent, came)
    whole = valid // 8 * 8
    for t in range(times):
        for c in range(2):
            for i in range(slab):
                base = (t * 2 + c) * valid * slab + i
                for level in range(0, whole, 8):
                    courant[t, c, i, level : level + 8, :] = raw[pl.ds(base + level * slab, 8, stride=slab), :]
                courant[t, c, i, whole:, :] = jnp.zeros((levels - whole, band), F32)
                for level in range(whole, valid):
                    row = base + level * slab
                    courant[t, c, i, level : level + 1, :] = raw[row : row + 1, :]
    collect(0, sent, came, target)
    post(1, weights, heavy)

    zero = jnp.zeros((8, band), F32)

    def begin(row, values, acc):
        put_state(0, row, values)
        for value in values:
            acc = acc + fold(value * value)
        store(s, row, values)
        store(p, row, values)
        return acc

    def norm(value):
        value = value.reshape(-1, 8, value.shape[-1]).sum(0)
        width = value.shape[-1]
        return sum(value[:, i : i + band] for i in range(0, width, band))

    def weigh_first(t):
        return scale[t] * seen[0, t]

    acc = adjoint(lambda t: target[t], begin, zero, True)
    collect(1, weights, heavy, scale)
    tangent(0)
    scalars = []

    def energy_first():
        total = zero
        for t in range(times):
            total = total + norm(weigh_first(t) * seen[0, t])
        return acc, total

    def imager(rho, energy):
        scalars.extend([rho, energy])

        def image(row, values, qq):
            outs = []
            for d, value in zip(load(p, row), values):
                q = d + value
                outs.append(q)
                qq = qq + fold(q * q)
            put_state(0, row, outs)
            store(s, row, outs)
            store(keep, row, outs)
            return qq

        return image

    qq = adjoint(weigh_first, imager, zero, True, 0, energy_first)
    first_leg(1, qq, zero)
    tangent(1, 1)
    rho, energy = scalars
    qq = totals(1)[0]
    pq = rho + energy
    alpha = rho / pq
    rho_new = rho - 2.0 * alpha * pq + alpha * alpha * qq
    beta = rho_new / rho
    grown = 1.0 + beta
    square = rho_new + beta * beta * rho

    def seen_next(t):
        return grown * seen[0, t] - alpha * seen[1, t]

    def weigh_next(t):
        return scale[t] * seen_next(t)

    def energy_next():
        total = zero
        for t in range(times):
            y = seen_next(t)
            total = total + norm(scale[t] * y * y)
        return total, zero

    def put_out(ref, row, values):
        var, level = divmod(row.start, levels)
        for low in range(0, TILE, 8):
            here = min(8, valid - level - low)
            for i, value in enumerate(values):
                base = (var * valid + level + low) * slab + i
                if here > 1:
                    ref[pl.ds(base, here, stride=slab), :] = value[low : low + here]
                elif here == 1:
                    ref[base : base + 1, :] = value[low : low + 1]

    def closer(energy, none):
        step = rho_new / (square + energy)

        def close(row, values, carry):
            first = load(p, row)
            image = load(keep, row)
            d = [grown * v - alpha * q for v, q in zip(first, image)]
            put_out(x_out, row, [alpha * v + step * w for v, w in zip(first, d)])
            residual = [v - alpha * q for v, q in zip(first, image)]
            put_out(r_out, row, [v - step * (w + z) for v, w, z in zip(residual, d, values)])
            return carry

        return close

    adjoint(weigh_next, closer, 0, False, 2, energy_next)


def pair_of(value):
    high = lax.reduce_precision(value, 8, 7)
    return high, lax.reduce_precision(value - high, 8, 7)


def body(courant, slot_column_cells, column_counts, innovations, error_weight, weighting):
    times, _, levels, slab, band = courant.shape
    owners, cap = slot_column_cells.shape[2:]
    chan = weighting.shape[1]
    slots = owners * cap
    lon_n, lat_n = lax.axis_size("lon"), lax.axis_size("lat")
    deep = -(-levels // 48) * 48

    field = courant.reshape(-1, band)
    weights = jnp.pad(weighting.reshape(2, levels, chan), ((0, 0), (0, deep - levels), (0, 0)))
    high, low = pair_of(weights)
    down_w = jnp.concatenate([high, low, high], axis=2).reshape(2 * deep, 3 * chan).astype(BF16)
    up_w = jnp.concatenate([high, low, high], axis=1).transpose(0, 2, 1).astype(BF16)
    position = lax.broadcasted_iota(jnp.int32, (times, cap, owners), 1)
    live = (position < column_counts[:, 0][:, None, :]).astype(F32).reshape(times, 1, slots)
    cells = slot_column_cells[:, 0].transpose(0, 2, 1).reshape(times, 1, slots)
    mail = (times, owners, cap, chan)

    state = (2 * deep, slab * band)
    vmem = pl.BlockSpec(memory_space=pltpu.VMEM)
    sums = 3
    x, r = pl.pallas_call(
        functools.partial(kernel, lon_n, lat_n, levels),
        out_shape=[jax.ShapeDtypeStruct((2 * levels * slab, band), F32)] * 2,
        in_specs=[vmem] * 7,
        out_specs=[vmem] * 2,
        scratch_shapes=[
            pltpu.VMEM((times, 2, slab, deep, band), F32),
            pltpu.VMEM((times, chan, slots), F32),
            pltpu.VMEM((times, chan, slots), F32),
            pltpu.VMEM(mail, F32),
            pltpu.VMEM(mail, F32),
            pltpu.VMEM(mail, F32),
            pltpu.VMEM(state, F32),
            pltpu.VMEM(state, F32),
            pltpu.VMEM(state, F32),
            pltpu.VMEM(state, F32),
            pltpu.VMEM((chan, slab * band), F32),
            pltpu.VMEM((3 * chan, slab * band), BF16),
            pltpu.VMEM((times, slab * band, slots), BF16),
            pltpu.VMEM((ITERS, times, chan, slots), F32),
            pltpu.VMEM((2, 4, 2 * deep, band), F32),
            pltpu.VMEM((2, 4, 2 * deep, band), F32),
            pltpu.VMEM((sums, 16, band), F32),
            pltpu.VMEM((sums, 16, band), F32),
            pltpu.VMEM((sums, lon_n, 16, band), F32),
            pltpu.VMEM((sums, lat_n, 16, band), F32),
            pltpu.SemaphoreType.DMA((2, CHUNKS, 4)),
            pltpu.SemaphoreType.DMA((2, CHUNKS, 4)),
            pltpu.SemaphoreType.DMA((sums, lon_n - 1)),
            pltpu.SemaphoreType.DMA((sums, lon_n - 1)),
            pltpu.SemaphoreType.DMA((sums, lat_n - 1)),
            pltpu.SemaphoreType.DMA((sums, lat_n - 1)),
            pltpu.SemaphoreType.DMA((2, owners - 1)),
            pltpu.SemaphoreType.DMA((2, owners - 1)),
        ],
        compiler_params=pltpu.CompilerParams(collective_id=0, has_side_effects=True, vmem_limit_bytes=48 * 2**20),
    )(field, cells, live, innovations[:, 0], error_weight[:, 0], up_w, down_w)

    def back(state):
        return state.reshape(2, levels, slab, band)

    return back(x), back(r)


def solution(mesh):
    owned = ("lon", "lat")
    in_specs = (
        P(None, None, None, "lon", "lat"),
        P(None, owned, None, None),
        P(None, owned, None),
        P(None, owned, None, None, None),
        P(None, owned, None, None, None),
        P(),
    )
    out_specs = (P(None, None, "lon", "lat"), P(None, None, "lon", "lat"))
    return jax.shard_map(body, mesh=mesh, in_specs=in_specs, out_specs=out_specs, check_vma=False)
```

```python
import functools

import jax
import jax.numpy as jnp
from jax import lax
from jax.experimental import pallas as pl
from jax.experimental.pallas import tpu as pltpu
from jax.sharding import PartitionSpec as P

ITERS = 2
CHUNKS = 4
TILE = 24
MESH = pl.DeviceIdType.MESH
F32 = jnp.float32
BF16 = jnp.bfloat16


def split(value):
    high = value.astype(BF16)
    return high, (value - high.astype(F32)).astype(BF16)


def dot(a, b):
    return jnp.dot(a, b, preferred_element_type=F32)


def dot_nt(a, b):
    return lax.dot_general(a, b, (((1,), (1,)), ((), ())), preferred_element_type=F32)


def kernel(
    lon_n, lat_n, valid,
    far_raw, cells, live, far_innovations, far_weights, far_weighting,
    x_out, r_out,
    raw, innovations, weights, weighting,
    courant, scale, target, sent, came, heavy, padded, up_w, down_w,
    p, s, keep, dep, y_acc, v_dep, onehot, seen,
    snd, rcv, part1, part2, sums1, sums2,
    ssem, rsem, s1, r1, s2, r2, asem, bsem, lsem,
):
    times, _, slab, levels, band = courant.shape
    count, cap = sent.shape[1:3]
    chan = weighting.shape[1]
    rows_h = 2 * levels // CHUNKS
    per_var = levels // rows_h
    a = lax.axis_index("lon")
    b = lax.axis_index("lat")
    peers = (
        (lax.rem(a + lon_n - 1, lon_n), b),
        (lax.rem(a + 1, lon_n), b),
        (a, lax.rem(b + lat_n - 1, lat_n)),
        (a, lax.rem(b + 1, lat_n)),
    )

    for par in range(2):
        for d in range(4):
            for var in range(2):
                tail = slice(var * levels + valid // 8 * 8, (var + 1) * levels)
                rcv[par, d, tail, :] = jnp.zeros((levels - valid // 8 * 8, band), F32)
    pairs = (
        (far_innovations, innovations),
        (far_weights, weights),
        (far_raw, raw),
        (far_weighting, weighting),
    )
    loads = [pltpu.make_async_copy(src, dst, lsem.at[n]) for n, (src, dst) in enumerate(pairs)]
    for one in loads:
        one.start()
    me = a * lat_n + b

    def place_of(off):
        other = lax.rem(me + off, count)
        return other, (other // lat_n, lax.rem(other, lat_n))

    barrier = pltpu.get_barrier_semaphore()

    def greet(off, none):
        pl.semaphore_signal(barrier, inc=1, device_id=place_of(off)[1], device_id_type=MESH)
        return none

    lax.fori_loop(1, count, greet, 0)

    lane = lax.broadcasted_iota(jnp.int32, (TILE, band), 1)
    has_south = (b > 0).astype(F32)
    has_north = (b < lat_n - 1).astype(F32)
    cols = [slice(i * band, (i + 1) * band) for i in range(slab)]

    def copies(par, h):
        span = pl.ds(h * rows_h, min(rows_h, valid - (h % per_var) * rows_h))
        return [
            pltpu.make_async_remote_copy(
                src_ref=snd.at[par, d, span],
                dst_ref=rcv.at[par, d, span],
                send_sem=ssem.at[par, h, d],
                recv_sem=rsem.at[par, h, d],
                device_id=peers[d],
                device_id_type=MESH,
            )
            for d in range(4)
        ]

    def start(par, h):
        for copy in copies(par, h):
            copy.start()

    def wait(par, h):
        for copy in copies(par, h):
            copy.wait()

    def tiles(h, body, carry=None):
        for n in range(rows_h // TILE):
            row = pl.ds(h * rows_h + n * TILE, TILE)
            crow = pl.ds((h % per_var) * rows_h + n * TILE, TILE)
            carry = body(row, crow, carry)
        return carry

    def winds(t, crow):
        return (
            [courant[t, 0, i, crow, :] for i in range(slab)],
            [courant[t, 1, i, crow, :] for i in range(slab)],
        )

    def load(ref, row):
        return [ref[row, c] for c in cols]

    def store(ref, row, values):
        for c, value in zip(cols, values):
            ref[row, c] = value

    def turn(value, shift):
        shift = shift % band
        return value if shift == 0 else pltpu.roll(value, shift, 1)

    def halos(par, row):
        from_south = rcv[par, 3, row, :] * has_south
        from_north = rcv[par, 2, row, :] * has_north
        return rcv[par, 1, row, :], rcv[par, 0, row, :], from_south, from_north

    def shifted(value, halo, i, up):
        if up:
            return jnp.where(lane == 0, turn(halo, -i), turn(value, 1))
        return jnp.where(lane == band - 1, turn(halo, slab - 1 - i), turn(value, -1))

    def advance(t, row, crow, par):
        u, v = winds(t, crow)
        x = load(s, row)
        west, east, south, north = halos(par, row)
        full = [west] + x + [east]
        outs = []
        for i in range(slab):
            out = (1.0 - jnp.abs(u[i]) - jnp.abs(v[i])) * x[i]
            out += jnp.maximum(u[i], 0.0) * full[i]
            out += jnp.maximum(-u[i], 0.0) * full[i + 2]
            out += jnp.maximum(v[i], 0.0) * shifted(x[i], south, i, True)
            out += jnp.maximum(-v[i], 0.0) * shifted(x[i], north, i, False)
            outs.append(out)
        return outs

    def retreat(t, row, crow, par):
        u, v = winds(t, crow)
        y = load(s, row)
        west, east, south, north = halos(par, row)
        plus = [jnp.maximum(u[i], 0.0) * y[i] for i in range(slab)] + [east]
        minus = [west] + [jnp.maximum(-u[i], 0.0) * y[i] for i in range(slab)]
        outs = []
        for i in range(slab):
            out = (1.0 - jnp.abs(u[i]) - jnp.abs(v[i])) * y[i]
            out += plus[i + 1] + minus[i]
            out += shifted(jnp.maximum(v[i], 0.0) * y[i], north, i, False)
            out += shifted(jnp.maximum(-v[i], 0.0) * y[i], south, i, True)
            outs.append(out)
        return outs

    def put_edges(par, row, west, east, southward, northward):
        snd[par, 0, row, :] = west
        snd[par, 1, row, :] = east
        low = jnp.zeros((TILE, band), F32)
        high = low
        for i in range(slab):
            low = jnp.where(lane == band - slab + i, turn(southward[i], band - slab + i), low)
            high = jnp.where(lane == i, turn(northward[i], i + 1), high)
        snd[par, 2, row, :] = low
        snd[par, 3, row, :] = high

    def put_state(par, row, x):
        put_edges(par, row, x[0], x[-1], x, x)

    def put_products(par, t, row, crow, y):
        u, v = winds(t, crow)
        put_edges(
            par, row,
            jnp.maximum(u[0], 0.0) * y[0],
            jnp.maximum(-u[-1], 0.0) * y[-1],
            [jnp.maximum(v[i], 0.0) * y[i] for i in range(slab)],
            [jnp.maximum(-v[i], 0.0) * y[i] for i in range(slab)],
        )

    def project(var):
        high, low = split(s[var * levels : (var + 1) * levels, :])
        y = dot(up_w[var], jnp.concatenate([high, high, low], axis=0))
        if var == 0:
            y_acc[...] = y
        else:
            y_acc[...] += y

    def scatter(t, weigh):
        pair = jnp.concatenate(split(weigh(t)), axis=0)
        both = dot_nt(pair, onehot[t])
        high, low = split(both[:chan] + both[chan:])
        v_dep[:chan, :] = high
        v_dep[chan : 2 * chan, :] = high
        v_dep[2 * chan :, :] = low

    def observe(k, t):
        pair = jnp.concatenate(split(y_acc[...]), axis=0)
        both = dot(pair, onehot[t])
        seen[k, t] = both[:chan] + both[chan:]

    def deposit(var, into):
        span = slice(var * levels, (var + 1) * levels)
        into[span, :] = dot(down_w[span, :], v_dep[...])

    def adjoint(weigh, finish, carry, pass_on, slot=None, partials=None, early=None):
        scatter(times - 1, weigh)
        for var in range(2):
            deposit(var, s)
            for h in range(var * per_var, (var + 1) * per_var):
                def enter(row, crow, none):
                    put_products(0, times - 1, row, crow, load(s, row))

                tiles(h, enter)
                start(0, h)
        if slot is not None:
            first_leg(slot, *partials())

        def step(n, none):
            t = times - 1 - n
            par = lax.rem(n, 2)
            if early is not None:
                pl.when(n == 0)(early)
            scatter(t - 1, weigh)
            for var in range(2):
                deposit(var, dep)
            if slot is not None:
                @pl.when(n == 1)
                def _():
                    second_leg(slot)

            for h in range(CHUNKS):
                wait(par, h)

                def back(row, crow, none):
                    y = [v + d for v, d in zip(retreat(t, row, crow, par), load(dep, row))]
                    store(s, row, y)
                    put_products(1 - par, t - 1, row, crow, y)

                tiles(h, back)
                start(1 - par, h)
            return none

        lax.fori_loop(0, times - 1, step, 0)
        if slot is not None:
            finish = finish(*totals(slot))
        par = (times - 1) % 2
        for h in range(CHUNKS):
            wait(par, h)

            def last(row, crow, carry):
                return finish(row, retreat(0, row, crow, par), carry)

            carry = tiles(h, last, carry)
            if pass_on:
                start(0, h)
        return carry

    def tangent(k, slot=None):
        def step(t, none):
            par = lax.rem(t, 2)
            if slot is not None:
                @pl.when(t == 1)
                def _():
                    second_leg(slot)

            for h in range(CHUNKS):
                wait(par, h)

                def onward(row, crow, none):
                    x = advance(t, row, crow, par)
                    store(s, row, x)
                    put_state(1 - par, row, x)

                tiles(h, onward)
                start(1 - par, h)
                if (h + 1) % per_var == 0:
                    project(h // per_var)
            observe(k, t)
            return none

        lax.fori_loop(0, times - 1, step, 0)
        par = (times - 1) % 2
        for h in range(CHUNKS):
            wait(par, h)

            def last(row, crow, none):
                store(s, row, advance(times - 1, row, crow, par))

            tiles(h, last)
            if (h + 1) % per_var == 0:
                project(h // per_var)
        observe(k, times - 1)

    def legs(k, axis):
        count, me, source, sums, send, receive = (
            (lon_n, a, part1, sums1, s1, r1),
            (lat_n, b, part2, sums2, s2, r2),
        )[axis]
        moves = []
        for off in range(1, count):
            other = lax.rem(me + off, count)
            moves.append(
                pltpu.make_async_remote_copy(
                    src_ref=source.at[k],
                    dst_ref=sums.at[k, me],
                    send_sem=send.at[k, off - 1],
                    recv_sem=receive.at[k, off - 1],
                    device_id=(other, b) if axis == 0 else (a, other),
                    device_id_type=MESH,
                )
            )
        return moves

    def launch(k, axis, tile):
        source, sums, me = ((part1, sums1, a), (part2, sums2, b))[axis]
        source[k] = tile
        sums[k, me] = tile
        for move in legs(k, axis):
            move.start()

    def land(k, axis):
        for move in legs(k, axis):
            move.wait()
        sums, count = ((sums1, lon_n), (sums2, lat_n))[axis]
        total = sums[k, 0]
        for j in range(1, count):
            total = total + sums[k, j]
        return total

    def first_leg(k, first, second):
        launch(k, 0, jnp.concatenate([first, second], axis=0))

    def second_leg(k):
        launch(k, 1, land(k, 0))

    def totals(k):
        tile = land(k, 1)
        return [jnp.sum(tile[8 * n : 8 * n + 8], keepdims=True) for n in range(2)]

    groups = ((times - 1, 1), (0, times - 1), (0, times))

    def parcel(which, source, landing, off):
        other, device = place_of(off)
        span = pl.ds(*groups[which])
        return pltpu.make_async_remote_copy(
            src_ref=source.at[span, other],
            dst_ref=landing.at[span, me],
            send_sem=asem.at[which, off - 1],
            recv_sem=bsem.at[which, off - 1],
            device_id=device,
            device_id_type=MESH,
        )

    def post(which, source, landing):
        first, length = groups[which]
        for t in range(first, first + length):
            landing[t, me] = source[t, me]

        def one(off, none):
            parcel(which, source, landing, off).start()
            return none

        lax.fori_loop(1, count, one, 0)

    def collect(which, source, landing, into):
        def one(off, none):
            parcel(which, source, landing, off).wait()
            return none

        lax.fori_loop(1, count, one, 0)
        first, length = groups[which]
        for t in range(first, first + length):
            rows = jnp.concatenate([landing[t, :, c, :] for c in range(cap)], axis=0)
            into[t] = rows.T * live[t]

    def fold(value):
        return value.reshape(TILE // 8, 8, band).sum(0)

    slots = cells.shape[-1]
    place = lax.broadcasted_iota(jnp.int32, (slab * band, slots), 0)
    for t in range(times):
        here = jnp.broadcast_to(cells[t], (slab * band, slots))
        onehot[t] = jnp.where(here == place, 1.0, 0.0).astype(BF16)
    loads[0].wait()
    loads[1].wait()
    for t in range(times):
        sent[t] = weights[t] * innovations[t]
    pl.semaphore_wait(barrier, count - 1)
    post(0, sent, came)
    post(1, sent, came)
    loads[2].wait()
    loads[3].wait()
    for var in range(2):
        padded[var] = jnp.zeros((levels, chan), F32)
        padded[var, :valid, :] = weighting[var * valid : (var + 1) * valid, :]
        high, low = split(padded[var])
        for n, part in enumerate((high, low, high)):
            down_w[var * levels : (var + 1) * levels, n * chan : (n + 1) * chan] = part
        high, low = split(padded[var].T)
        up_w[var] = jnp.concatenate([high, low, high], axis=1)
    whole = valid // 8 * 8
    for t in range(times):
        for c in range(2):
            for i in range(slab):
                base = (t * 2 + c) * valid * slab + i
                for level in range(0, whole, 8):
                    courant[t, c, i, level : level + 8, :] = raw[pl.ds(base + level * slab, 8, stride=slab), :]
                courant[t, c, i, whole:, :] = jnp.zeros((levels - whole, band), F32)
                for level in range(whole, valid):
                    row = base + level * slab
                    courant[t, c, i, level : level + 1, :] = raw[row : row + 1, :]
    collect(0, sent, came, target)

    def rest():
        collect(1, sent, came, target)
        post(2, weights, heavy)


    zero = jnp.zeros((8, band), F32)

    def begin(row, values, acc):
        put_state(0, row, values)
        for value in values:
            acc = acc + fold(value * value)
        store(s, row, values)
        store(p, row, values)
        return acc

    def norm(value):
        value = value.reshape(-1, 8, value.shape[-1]).sum(0)
        width = value.shape[-1]
        return sum(value[:, i : i + band] for i in range(0, width, band))

    def weigh_first(t):
        return scale[t] * seen[0, t]

    acc = adjoint(lambda t: target[t], begin, zero, True, early=rest)
    collect(2, weights, heavy, scale)
    tangent(0)
    scalars = []

    def energy_first():
        total = zero
        for t in range(times):
            total = total + norm(weigh_first(t) * seen[0, t])
        return acc, total

    def imager(rho, energy):
        scalars.extend([rho, energy])

        def image(row, values, qq):
            outs = []
            for d, value in zip(load(p, row), values):
                q = d + value
                outs.append(q)
                qq = qq + fold(q * q)
            put_state(0, row, outs)
            store(s, row, outs)
            store(keep, row, outs)
            return qq

        return image

    qq = adjoint(weigh_first, imager, zero, True, 0, energy_first)
    first_leg(1, qq, zero)
    tangent(1, 1)
    rho, energy = scalars
    qq = totals(1)[0]
    pq = rho + energy
    alpha = rho / pq
    rho_new = rho - 2.0 * alpha * pq + alpha * alpha * qq
    beta = rho_new / rho
    grown = 1.0 + beta
    square = rho_new + beta * beta * rho

    def seen_next(t):
        return grown * seen[0, t] - alpha * seen[1, t]

    def weigh_next(t):
        return scale[t] * seen_next(t)

    def energy_next():
        total = zero
        for t in range(times):
            y = seen_next(t)
            total = total + norm(scale[t] * y * y)
        return total, zero

    def put_out(ref, row, values):
        var, level = divmod(row.start, levels)
        for low in range(0, TILE, 8):
            here = min(8, valid - level - low)
            for i, value in enumerate(values):
                base = (var * valid + level + low) * slab + i
                if here > 1:
                    ref[pl.ds(base, here, stride=slab), :] = value[low : low + here]
                elif here == 1:
                    ref[base : base + 1, :] = value[low : low + 1]

    def closer(energy, none):
        step = rho_new / (square + energy)

        def close(row, values, carry):
            first = load(p, row)
            image = load(keep, row)
            d = [grown * v - alpha * q for v, q in zip(first, image)]
            put_out(x_out, row, [alpha * v + step * w for v, w in zip(first, d)])
            residual = [v - alpha * q for v, q in zip(first, image)]
            put_out(r_out, row, [v - step * (w + z) for v, w, z in zip(residual, d, values)])
            return carry

        return close

    adjoint(weigh_next, closer, 0, False, 2, energy_next)


def body(courant, slot_column_cells, column_counts, innovations, error_weight, weighting):
    times, _, levels, slab, band = courant.shape
    owners, cap = slot_column_cells.shape[2:]
    chan = weighting.shape[1]
    slots = owners * cap
    lon_n, lat_n = lax.axis_size("lon"), lax.axis_size("lat")
    deep = -(-levels // 48) * 48

    field = courant.reshape(-1, band)
    position = lax.broadcasted_iota(jnp.int32, (times, cap, owners), 1)
    live = (position < column_counts[:, 0][:, None, :]).astype(F32).reshape(times, 1, slots)
    cells = slot_column_cells[:, 0].transpose(0, 2, 1).reshape(times, 1, slots)
    mail = (times, owners, cap, chan)

    state = (2 * deep, slab * band)
    vmem = pl.BlockSpec(memory_space=pltpu.VMEM)
    far = pl.BlockSpec(memory_space=pltpu.HBM)
    sums = 3
    x, r = pl.pallas_call(
        functools.partial(kernel, lon_n, lat_n, levels),
        out_shape=[jax.ShapeDtypeStruct((2 * levels * slab, band), F32)] * 2,
        in_specs=[far, vmem, vmem, far, far, far],
        out_specs=[vmem] * 2,
        scratch_shapes=[
            pltpu.VMEM(field.shape, F32),
            pltpu.VMEM(mail, F32),
            pltpu.VMEM(mail, F32),
            pltpu.VMEM(weighting.shape, F32),
            pltpu.VMEM((times, 2, slab, deep, band), F32),
            pltpu.VMEM((times, chan, slots), F32),
            pltpu.VMEM((times, chan, slots), F32),
            pltpu.VMEM(mail, F32),
            pltpu.VMEM(mail, F32),
            pltpu.VMEM(mail, F32),
            pltpu.VMEM((2, deep, chan), F32),
            pltpu.VMEM((2, chan, 3 * deep), BF16),
            pltpu.VMEM((2 * deep, 3 * chan), BF16),
            pltpu.VMEM(state, F32),
            pltpu.VMEM(state, F32),
            pltpu.VMEM(state, F32),
            pltpu.VMEM(state, F32),
            pltpu.VMEM((chan, slab * band), F32),
            pltpu.VMEM((3 * chan, slab * band), BF16),
            pltpu.VMEM((times, slab * band, slots), BF16),
            pltpu.VMEM((ITERS, times, chan, slots), F32),
            pltpu.VMEM((2, 4, 2 * deep, band), F32),
            pltpu.VMEM((2, 4, 2 * deep, band), F32),
            pltpu.VMEM((sums, 16, band), F32),
            pltpu.VMEM((sums, 16, band), F32),
            pltpu.VMEM((sums, lon_n, 16, band), F32),
            pltpu.VMEM((sums, lat_n, 16, band), F32),
            pltpu.SemaphoreType.DMA((2, CHUNKS, 4)),
            pltpu.SemaphoreType.DMA((2, CHUNKS, 4)),
            pltpu.SemaphoreType.DMA((sums, lon_n - 1)),
            pltpu.SemaphoreType.DMA((sums, lon_n - 1)),
            pltpu.SemaphoreType.DMA((sums, lat_n - 1)),
            pltpu.SemaphoreType.DMA((sums, lat_n - 1)),
            pltpu.SemaphoreType.DMA((3, owners - 1)),
            pltpu.SemaphoreType.DMA((3, owners - 1)),
            pltpu.SemaphoreType.DMA((4,)),
        ],
        compiler_params=pltpu.CompilerParams(collective_id=0, has_side_effects=True, vmem_limit_bytes=56 * 2**20),
    )(field, cells, live, innovations[:, 0], error_weight[:, 0], weighting)

    def back(state):
        return state.reshape(2, levels, slab, band)

    return back(x), back(r)


def solution(mesh):
    owned = ("lon", "lat")
    in_specs = (
        P(None, None, None, "lon", "lat"),
        P(None, owned, None, None),
        P(None, owned, None),
        P(None, owned, None, None, None),
        P(None, owned, None, None, None),
        P(),
    )
    out_specs = (P(None, None, "lon", "lat"), P(None, None, "lon", "lat"))
    return jax.shard_map(body, mesh=mesh, in_specs=in_specs, out_specs=out_specs, check_vma=False)
```
